32 devices in a mesh: tile: 2 (over x), gx: 16 (over z, y, core).
Axes of the slice: x: 2, y: 2, z: 4, core: 2. Of those that a mesh axis runs over, the one named last changes fastest.
Arguments:
- points: bfloat16 [524288, 192], P(('tile', 'gx')), parts along dimension 0, may hold values from -6 to 6
- gain: float32 [192], replicated, may hold values from 0.1 to 1.9
- w_qkv: bfloat16 [192, 576], replicated
- w_out: bfloat16 [192, 192], replicated, may hold values from -1.75 to 1.75
- counts: int32 [4096], P(('tile', 'gx')), parts along dimension 0, may hold values from 32 to 128, as said below
- far_index: int32 [4096, 128], P(('tile', 'gx')), parts along dimension 0, may hold values from 0 to 2175, as said below
Outputs:
- attended: bfloat16 [524288, 192], P(('tile', 'gx')), parts along dimension 0
The draws below stay inside these ranges and needn't reach their ends.
There are 2 independent parts, one for each index of `tile`. The reference program is written for one: setup_inputs(seed, part) draws one part's arguments, and reference() takes and returns one part's arrays. A program takes and returns all parts, laid end to end along the dimension named above; an argument that names none is the same for every part. Nothing has to cross between parts.
Inputs may be any that keep to these rules, and one draw needn't show every extreme that they name: `counts`: every window of a tile has between 32 and 128 live points and some window has exactly 128. w * 128 - 1024 + far_index[w, :] names live point slots of windows whose rows lie within 1024 rows before the start or after the end of window w, inside the tile.
All inputs are finite; a program needn't handle non-finite values.
Results may differ from the reference program's by a relative error of at most 0.002.
The reference program's roundings to bfloat16 on the way (of `normed`, `qkv`, `prob` and `mixed`) count: a program that leaves them out, or rounds other values in their place, can miss the bound.
Values may be sent and summed in bfloat16 or wider, within the bound.
No kernel may reach another device: no remote copies, remote signals or barrier semaphores. Data moves between devices by JAX's collectives and lax.ppermute only.
A program may use at most 192 MiB of HBM per device.

```python
import math
import jax
import jax.numpy as jnp
from jax import lax

C = 192
HEADS = 6
WIN = 128
FAR = 128
REACH = 1024
POINTS = 262144
WINDOWS = 2048


def window_counts(key):
    sub = jax.random.fold_in(key, 11)
    live = jax.random.randint(sub, (WINDOWS,), 32, WIN + 1)
    chosen = jax.random.randint(jax.random.fold_in(key, 12), (), 0, WINDOWS)
    return live.at[chosen].set(WIN).astype(jnp.int32)


def draw_counts(key, part):
    return window_counts(key)


def draw_far_index(key, part):
    live = window_counts(key)
    windows = jnp.arange(WINDOWS, dtype=jnp.int32)
    start = windows * WIN
    low_row = jnp.maximum(start - REACH, 0)
    high_row = jnp.minimum(start + WIN + REACH, POINTS)
    low_win = low_row // WIN
    spread = (high_row - low_row) // WIN
    pick = jax.random.randint(jax.random.fold_in(key, 21), (WINDOWS, FAR), 0, 1 << 20)
    target = low_win[:, None] + pick % spread[:, None]
    slotpick = jax.random.randint(jax.random.fold_in(key, 22), (WINDOWS, FAR), 0, 1 << 20)
    slot = slotpick % live[target]
    return (target * WIN + slot - (start[:, None] - REACH)).astype(jnp.int32)


def draw_w_qkv(key, part):
    values = jax.random.normal(key, (C, 3 * C), jnp.float32) / jnp.sqrt(jnp.float32(C))
    return values.astype(jnp.bfloat16)


def shard_levels(stream_key, extent, split, low, high):
    factor_of, own = 1.0, jax.random.fold_in(stream_key, 6)
    for axis_at, blocks in split:
        steps = jnp.exp(jax.random.uniform(jax.random.fold_in(own, axis_at), (blocks,), jnp.float32, low / len(split), high / len(split)))
        factor_of = factor_of * jnp.repeat(steps, extent[axis_at] // blocks).reshape([-1 if axis == axis_at else 1 for axis in range(len(extent))])
    return factor_of


def centred(own_key, dims, scale, reach, shards=(), kind=jnp.bfloat16):
    drawn = jax.random.normal(own_key, dims, jnp.float32) * scale
    if len(shards) > 0:
        drawn = shard_levels(own_key, dims, shards, -0.22, 0.18) * drawn
    return jnp.clip(drawn, min=-reach, max=reach).astype(kind)


def setup_inputs(seed: int = 0, part: int = 0) -> dict:
    streams_of = jax.random.split(jax.random.key(seed), 7)
    part_splits = jax.random.split(jax.random.fold_in(streams_of[6], part), 7)
    points = centred(part_splits[0], (POINTS, C), 1.0, 6.0, ((0, 16),))
    gain = jnp.clip(1.0 + 0.18 * jax.random.normal(streams_of[1], (C,), jnp.float32), 0.1, 1.9)
    w_qkv = draw_w_qkv(jax.random.fold_in(streams_of[6], 71), part)
    w_out = centred(streams_of[3], (C, C), (C // 16) ** -0.5, 1.75)
    counts = draw_counts(jax.random.fold_in(jax.random.fold_in(streams_of[6], part), 71), part)
    far_index = draw_far_index(jax.random.fold_in(jax.random.fold_in(streams_of[6], part), 71), part)
    return {"points": points, "gain": gain, "w_qkv": w_qkv, "w_out": w_out, "counts": counts, "far_index": far_index}


def attend_windows(queries, dense_kv, far_kv, live):
    group, slots, width = queries.shape
    head_dim = width // HEADS
    far_count = far_kv.shape[1]
    qh = queries.astype(jnp.float32).reshape(group, slots, HEADS, head_dim)
    allkv = jnp.concatenate([dense_kv, far_kv], axis=1).astype(jnp.float32)
    keys = allkv[..., :width].reshape(group, slots + far_count, HEADS, head_dim)
    values = allkv[..., width:].reshape(group, slots + far_count, HEADS, head_dim)
    scores = jnp.einsum('gqhd,gkhd->ghqk', qh, keys) / math.sqrt(head_dim)
    valid = jnp.concatenate([jnp.arange(slots)[None, :] < live[:, None], jnp.ones((group, far_count), bool)], axis=1)
    scores = jnp.where(valid[:, None, None, :], scores, jnp.float32(-1e+30))
    top = lax.optimization_barrier(jnp.max(scores, axis=-1, keepdims=True))
    expo = jnp.exp(scores - top)
    prob = (expo / lax.optimization_barrier(jnp.sum(expo, axis=-1, keepdims=True))).astype(jnp.bfloat16)
    mixed = jnp.einsum('ghqk,gkhd->gqhd', prob.astype(jnp.float32), values)
    return mixed.reshape(group, slots, width).astype(jnp.bfloat16)

def reference(points, gain, w_qkv, w_out, counts, far_index):
    width = points.shape[1]
    xf = points.astype(jnp.float32)
    mean = lax.optimization_barrier(jnp.mean(xf, axis=1, keepdims=True))
    var = lax.optimization_barrier(jnp.mean((xf - mean) ** 2, axis=1, keepdims=True))
    normed = ((xf - mean) / jnp.sqrt(var + 1e-05) * gain).astype(jnp.bfloat16)
    qkv = jnp.dot(normed, w_qkv, preferred_element_type=jnp.float32).astype(jnp.bfloat16)
    queries = qkv[:, :width]
    keyvals = qkv[:, width:]
    starts = (jnp.arange(WINDOWS, dtype=jnp.int32) * WIN - REACH).astype(jnp.int32)
    absolute = (far_index + starts[:, None]).astype(jnp.int32)
    group = math.gcd(WINDOWS, 64)
    blocks = WINDOWS // group
    q4 = queries.reshape(blocks, group, WIN, width)
    kv4 = keyvals.reshape(blocks, group, WIN, 2 * width)
    idx = absolute.reshape(blocks, group * FAR)
    live = counts.reshape(blocks, group)

    def one_block(items):
        qb, kvb, ib, lb = items
        farkv = jnp.take(keyvals, ib, axis=0).reshape(group, FAR, 2 * width)
        return attend_windows(qb, kvb, farkv, lb)
    mixed = lax.map(one_block, (q4, kv4, idx, live)).reshape(POINTS, width)
    return jnp.dot(mixed, w_out, preferred_element_type=jnp.float32).astype(jnp.bfloat16)
```

```python
import functools
import math

import jax
import jax.numpy as jnp
from jax import lax
from jax.experimental import pallas as pl
from jax.experimental.pallas import tpu as pltpu
from jax.sharding import PartitionSpec as P

HEADS = 6
WIN = 128
REACH = 1024
LANES = 128
PARTS = 4
BIAS = 64
DEAD = -1e30


def project(x, row, live, gain, wq, wkv, store, queries=None, column=None):
    xf = x.astype(jnp.float32)
    width, size = xf.shape
    mean = jnp.sum(xf, axis=0, keepdims=True) / width
    centred = xf - mean
    var = jnp.sum(centred * centred, axis=0, keepdims=True) / width
    scale = 1.0 / jnp.sqrt(var + 1e-05)
    normed = (centred * scale * gain).astype(jnp.bfloat16)
    if queries is not None:
        q = jnp.dot(wq, normed, preferred_element_type=jnp.float32)
        queries[:, pl.ds(column, size)] = q.astype(jnp.bfloat16)
    kv = lax.dot_general(
        normed, wkv, (((0,), (0,)), ((), ())), preferred_element_type=jnp.float32
    )
    kv = kv.astype(jnp.bfloat16).astype(jnp.float32)
    for part in range(PARTS):
        piece = kv[:, part * LANES : (part + 1) * LANES]
        if part == 1 and live is not None:
            lane = lax.broadcasted_iota(jnp.int32, (WIN, LANES), 1)
            slot = lax.broadcasted_iota(jnp.int32, (WIN, LANES), 0)
            bias = [
                jnp.where((lane == BIAS) & (slot >= count), DEAD, 0.0) for count in live
            ]
            piece = piece + jnp.concatenate(bias, axis=0)
        store[pl.ds(row * PARTS + part, size, stride=PARTS), :] = piece


def prepare(window, far_ref, store, far_rows, spread, queries, width):
    head_dim = width // HEADS
    for j in range(WIN):
        at = far_ref[window, j]
        far_rows[pl.ds(j * PARTS, PARTS), :] = store[
            pl.ds(pl.multiple_of(at * PARTS, PARTS), PARTS), :
        ]
    own = (window * WIN + REACH) * PARTS
    pieces = []
    for part in range(PARTS):
        dense = store[pl.ds(own + part, WIN, stride=PARTS), :]
        far = far_rows[pl.ds(part, WIN, stride=PARTS), :]
        pieces.append(jnp.concatenate([dense, far], axis=0))
    keys = jnp.concatenate([pieces[0], pieces[1]], axis=1).astype(jnp.bfloat16)
    values = jnp.concatenate(
        [pieces[2].T.astype(jnp.bfloat16), pieces[3].T[: LANES // 2].astype(jnp.bfloat16)],
        axis=0,
    )
    q = queries[:, pl.ds(pl.multiple_of(window * WIN, WIN), WIN)]
    for h in range(HEADS):
        spread[pl.ds(h * head_dim, head_dim), pl.ds(h * WIN, WIN)] = q[
            h * head_dim : (h + 1) * head_dim
        ]
    return keys, values


HP = 2


def scores(keys, spread, item):
    return jnp.dot(
        keys,
        spread[:, pl.ds(item * HP * WIN, HP * WIN)],
        preferred_element_type=jnp.float32,
    )


def soft(s2, head_dim):
    factor = math.log2(math.e) / math.sqrt(head_dim)
    top = jnp.max(s2, axis=0, keepdims=True)
    expo = jnp.exp2((s2 - top) * factor)
    inverse = 1.0 / jnp.sum(expo, axis=0, keepdims=True)
    return (expo * inverse).astype(jnp.bfloat16)


def mix(values, prob, item, head_dim):
    out = jnp.dot(
        values[item * HP * head_dim : (item + 1) * HP * head_dim],
        prob,
        preferred_element_type=jnp.float32,
    )
    return [out[i * head_dim : (i + 1) * head_dim, i * WIN : (i + 1) * WIN] for i in range(HP)]


def attend_group(first, group, far_ref, store, far_rows, spread, queries, w_out, width, out):
    head_dim = width // HEADS
    per = HEADS // HP
    items = [(i, p) for i in range(group) for p in range(per)]
    ready, pending, probs, mixed = {}, {}, {}, {}

    def get_ready(n):
        i, p = items[n]
        if p == 0:
            ready[i] = prepare(first + i, far_ref, store, far_rows.at[i], spread.at[i], queries, width)

    def score(n):
        i, p = items[n]
        pending[n] = scores(ready[i][0], spread.at[i], p)

    def blend(n):
        i, p = items[n]
        mixed.setdefault(i, []).extend(mix(ready[i][1], probs.pop(n), p, head_dim))

    def finish(n):
        i, p = items[n]
        if p == per - 1:
            m = jnp.concatenate(mixed.pop(i), axis=0).astype(jnp.bfloat16)
            out[:, i * WIN : (i + 1) * WIN] = jnp.dot(
                w_out, m, preferred_element_type=jnp.float32).astype(jnp.bfloat16)

    def softmax(n):
        probs[n] = soft(pending.pop(n), head_dim)

    stages = ((get_ready, 0), (score, PREP), (softmax, PREP + AHEAD), (blend, PREP + AHEAD + BEHIND), (finish, PREP + AHEAD + BEHIND + TAIL))
    for n in range(len(items) + stages[-1][1]):
        for run, late in stages:
            if 0 <= n - late < len(items):
                run(n - late)


AHEAD, BEHIND, PREP, TAIL = 3,2,3,1


def body(
    steps, block, group, far_ref, live_ref, low, own, high, gain, wq, wkv, w_out, out,
    store, queries, far_rows, spread,
):
    low_steps, own_steps, high_steps = steps
    width = own.shape[0]
    step = pl.program_id(0)
    per = block // WIN

    @pl.when(step == 0)
    def _():
        for slot in range(group):
            spread[slot, :, :] = jnp.zeros(spread.shape[1:], spread.dtype)
            spread[slot, LANES + BIAS : LANES + BIAS + 16, :] = jnp.where(
                lax.broadcasted_iota(jnp.int32, (16, spread.shape[2]), 0) == 0, 1.0, 0.0
            ).astype(spread.dtype)

    row = pl.multiple_of(step * block, block)

    @pl.when(step < low_steps)
    def _():
        project(low[...], row, None, gain[...], wq[...], wkv[...], store)

    @pl.when((step >= low_steps) & (step < low_steps + own_steps))
    def _():
        first = (step - low_steps) * per
        live = [live_ref[first + i] for i in range(per)]
        column = pl.multiple_of((step - low_steps) * block, block)
        project(
            own[...], row, live, gain[...], wq[...], wkv[...], store, queries, column
        )

    @pl.when((step >= low_steps + own_steps) & (step < sum(steps)))
    def _():
        project(high[...], row, None, gain[...], wq[...], wkv[...], store)

    @pl.when(step >= sum(steps))
    def _():
        first = (step - sum(steps)) * group
        attend_group(first, group, far_ref, store, far_rows, spread, queries, w_out[...], width, out)


def local(points, low, high, gain, wq, wkv, w_out, counts, far, block=512, group=8):
    width, rows = points.shape
    reach = low.shape[1]
    windows = rows // WIN
    steps = (reach // block, rows // block, reach // block)
    before = sum(steps)
    total = rows + 2 * reach
    whole = lambda shape: pl.BlockSpec(shape, lambda t, *_: (0, 0))
    last = lambda t, start, count: (0, jnp.clip(t - start, 0, count - 1))
    return pl.pallas_call(
        functools.partial(body, steps, block, group),
        out_shape=jax.ShapeDtypeStruct((width, rows), jnp.bfloat16),
        grid_spec=pltpu.PrefetchScalarGridSpec(
            num_scalar_prefetch=2,
            grid=(before + windows // group,),
            in_specs=[
                pl.BlockSpec((width, block), lambda t, *_: last(t, 0, steps[0])),
                pl.BlockSpec((width, block), lambda t, *_: last(t, steps[0], steps[1])),
                pl.BlockSpec(
                    (width, block), lambda t, *_: last(t, steps[0] + steps[1], steps[2])
                ),
                whole(gain.shape),
                whole(wq.shape),
                whole(wkv.shape),
                whole(w_out.shape),
            ],
            out_specs=pl.BlockSpec(
                (width, group * WIN), lambda t, *_: (0, jnp.maximum(t - before, 0))
            ),
            scratch_shapes=[
                pltpu.VMEM((total * PARTS, LANES), jnp.float32),
                pltpu.VMEM((width, rows), jnp.bfloat16),
                pltpu.VMEM((group, WIN * PARTS, LANES), jnp.float32),
                pltpu.VMEM((group, 2 * LANES, HEADS * WIN), jnp.bfloat16),
            ],
        ),
        compiler_params=pltpu.CompilerParams(vmem_limit_bytes=60 << 20),
    )(far, counts, low, points, high, gain, wq, wkv, w_out)


def weights(w_qkv, w_out, width):
    head_dim = width // HEADS
    cut = LANES // head_dim * head_dim
    wq = w_qkv[:, :width].T
    k, v = w_qkv[:, width : 2 * width], w_qkv[:, 2 * width :]
    pad = jnp.zeros((width, 2 * LANES - width), w_qkv.dtype)
    wkv = jnp.concatenate([k[:, :cut], k[:, cut:], pad, v[:, :cut], v[:, cut:], pad], axis=1)
    return wq, wkv, w_out.T


def shards(points, gain, w_qkv, w_out, counts, far_index):
    rows, width = points.shape
    x = points.T
    count = lax.axis_size("gx")
    forward = [(i, i + 1) for i in range(count - 1)]
    backward = [(i + 1, i) for i in range(count - 1)]
    low = lax.ppermute(x[:, rows - REACH :], "gx", forward)
    high = lax.ppermute(x[:, :REACH], "gx", backward)
    windows = rows // WIN
    far = far_index + (jnp.arange(windows, dtype=jnp.int32) * WIN)[:, None]
    wq, wkv, wo = weights(w_qkv, w_out, width)
    out = local(x, low, high, gain[:, None], wq, wkv, wo, counts, far)
    return out.T


def solution(mesh):
    return jax.shard_map(
        shards,
        mesh=mesh,
        in_specs=(
            P(("tile", "gx"), None),
            P(),
            P(),
            P(),
            P(("tile", "gx")),
            P(("tile", "gx"), None),
        ),
        out_specs=P(("tile", "gx"), None),
        check_vma=False,
    )
```

```python
import functools
import math

import jax
import jax.numpy as jnp
from jax import lax
from jax.experimental import pallas as pl
from jax.experimental.pallas import tpu as pltpu
from jax.sharding import PartitionSpec as P

HEADS = 6
WIN = 128
REACH = 1024
LANES = 128
PARTS = 4
PAD = 2 * PARTS
BIAS = 64
DEAD = -1e30
BLOCK = 1024
SUB = 256
GROUP = 16
SLOTS = 4
PAIR = 2
EARLY, PREP, AHEAD, BEHIND, TAIL = 4, 3, 3, 3, 2


def pipelined(count, stages):
    for n in range(count + max(lag for _, lag in stages)):
        for run, lag in stages:
            if 0 <= n - lag < count:
                run(n - lag)


def project(xq, column, gain, wq, wkv, store, live=None, queries=True):
    width = xq.shape[0]
    norms, dots = {}, {}

    def norm(n):
        xf = xq[:, pl.ds(column + n * SUB, SUB)].astype(jnp.float32)
        mean = jnp.sum(xf, axis=0, keepdims=True) / width
        centred = xf - mean
        var = jnp.sum(centred * centred, axis=0, keepdims=True) / width
        scale = 1.0 / jnp.sqrt(var + 1e-05)
        full = jnp.concatenate([gain[...]] * (SUB // LANES), axis=1)
        norms[n] = (centred * scale * full).astype(jnp.bfloat16)

    def dot(n):
        normed = norms.pop(n)
        q = None
        if queries:
            q = jnp.dot(wq[...], normed, preferred_element_type=jnp.float32)
        kv = lax.dot_general(
            normed, wkv[...], (((0,), (0,)), ((), ())), preferred_element_type=jnp.float32
        )
        dots[n] = q, kv

    def keep(n):
        q, kv = dots.pop(n)
        if queries:
            xq[:, pl.ds(column + n * SUB, SUB)] = q.astype(jnp.bfloat16)
        kv = kv.astype(jnp.bfloat16).astype(jnp.float32)
        for part in range(PARTS):
            piece = kv[:, part * LANES : (part + 1) * LANES]
            if part == 1 and live is not None:
                lane = lax.broadcasted_iota(jnp.int32, (WIN, LANES), 1)
                slot = lax.broadcasted_iota(jnp.int32, (WIN, LANES), 0)
                bias = [
                    jnp.where((lane == BIAS) & (slot >= live(n * SUB // WIN + i)), DEAD, 0.0)
                    for i in range(SUB // WIN)
                ]
                piece = piece + jnp.concatenate(bias, axis=0)
            store[pl.ds(PAD + (column + n * SUB) * PARTS + part, SUB, stride=PARTS), :] = piece

    pipelined(BLOCK // SUB, ((norm, 0), (dot, 1), (keep, 2)))


def attend(column, window, far_ref, xq, w_out, store, far_rows, spread):
    width = xq.shape[0]
    head_dim = width // HEADS
    factor = math.log2(math.e) / math.sqrt(head_dim)
    per = HEADS // PAIR
    ready, pending, probs, mixed = {}, {}, {}, {}

    def gather(n):
        i, p = divmod(n, per)
        base = (pl.multiple_of(column + i * WIN, WIN) - REACH) * PARTS
        rows = far_rows.at[i % SLOTS]
        upper = lax.broadcasted_iota(jnp.int32, (2 * PARTS, LANES), 0) >= PARTS
        for j in range(p * WIN // per // 2 * 2, (p + 1) * WIN // per // 2 * 2, 2):
            one, two = [
                store[pl.ds(pl.multiple_of(at, PARTS), 2 * PARTS), :]
                for at in (
                    base + PAD + far_ref[window + i, j] * PARTS,
                    base + PAD - PARTS + far_ref[window + i, j + 1] * PARTS,
                )
            ]
            rows[pl.ds(j * PARTS, 2 * PARTS), :] = jnp.where(upper, two, one)

    def prepare(n):
        if n % per:
            return
        i = n // per
        own = pl.multiple_of(column + i * WIN, WIN)
        rows = far_rows.at[i % SLOTS]
        pieces = []
        for part in range(PARTS):
            dense = store[pl.ds(PAD + own * PARTS + part, WIN, stride=PARTS), :]
            far = rows[pl.ds(part, WIN, stride=PARTS), :]
            pieces.append(jnp.concatenate([dense, far], axis=0))
        keys = jnp.concatenate(pieces[:2], axis=1).astype(jnp.bfloat16)
        values = [pieces[2].T, pieces[3].T[: width - LANES]]
        values = jnp.concatenate(values, axis=0).astype(jnp.bfloat16)
        q = xq[:, pl.ds(own, WIN)]
        for h in range(HEADS):
            head = slice(h * head_dim, (h + 1) * head_dim)
            spread[i % SLOTS, head, h * WIN : (h + 1) * WIN] = q[head]
        ready[i] = keys, values

    def score(n):
        i, p = divmod(n, per)
        pending[n] = jnp.dot(
            ready[i][0],
            spread[i % SLOTS, :, p * PAIR * WIN : (p + 1) * PAIR * WIN],
            preferred_element_type=jnp.float32,
        )

    def softmax(n):
        s2 = pending.pop(n)
        halves = []
        for h in range(PAIR):
            s = s2[:, h * WIN : (h + 1) * WIN]
            top = jnp.max(s, axis=0, keepdims=True)
            expo = jnp.exp2((s - top) * factor)
            inverse = 1.0 / jnp.sum(expo, axis=0, keepdims=True)
            halves.append((expo * inverse).astype(jnp.bfloat16))
        probs[n] = jnp.concatenate(halves, axis=1)

    def blend(n):
        i, p = divmod(n, per)
        out = jnp.dot(
            ready[i][1][p * PAIR * head_dim : (p + 1) * PAIR * head_dim],
            probs.pop(n),
            preferred_element_type=jnp.float32,
        )
        for h in range(PAIR):
            piece = out[h * head_dim : (h + 1) * head_dim, h * WIN : (h + 1) * WIN]
            mixed.setdefault(i, []).append(piece)

    def finish(n):
        i, p = divmod(n, per)
        if p < per - 1:
            return
        m = jnp.concatenate(mixed.pop(i), axis=0).astype(jnp.bfloat16)
        out = jnp.dot(w_out[...], m, preferred_element_type=jnp.float32)
        xq[:, pl.ds(column + i * WIN, WIN)] = out.astype(jnp.bfloat16)

    lags = [EARLY, PREP, AHEAD, BEHIND, TAIL]
    lags = [sum(lags[:i]) for i in range(6)]
    pipelined(GROUP * per, tuple(zip((gather, prepare, score, softmax, blend, finish), lags)))


def arrange(gain, w_qkv, w_out, full_gain, wq, wkv, wo):
    width = w_qkv.shape[0]
    f32 = jnp.float32
    full_gain[...] = jnp.broadcast_to(gain[...], (LANES, width)).T
    w = w_qkv[...].astype(f32)
    wq[...] = w[:, :width].T.astype(wq.dtype)
    wo[...] = w_out[...].astype(f32).T.astype(wo.dtype)
    pad = jnp.zeros((width, 2 * LANES - width), f32)
    parts = []
    for first in (width, 2 * width):
        parts += [w[:, first : first + width], pad]
    wkv[...] = jnp.concatenate(parts, axis=1).astype(wkv.dtype)


def body(
    far_ref, live_ref, x, low, high, gain, w_qkv, w_out, out,
    store, xq, far_rows, spread, full_gain, wq, wkv, wo, got, sent,
):
    width, rows = x.shape
    reach = low.shape[1]
    halo, main = reach // BLOCK, rows // BLOCK

    def fetch(src, at, column, size, slot):
        return pltpu.make_async_copy(
            src.at[:, pl.ds(at, size)], xq.at[:, pl.ds(column, size)], got.at[slot]
        )

    copies = [fetch(x, i * BLOCK, reach + i * BLOCK, BLOCK, i) for i in range(main)]
    copies += [fetch(low, i * BLOCK, i * BLOCK, BLOCK, main + i) for i in range(halo)]
    copies += [
        fetch(high, i * BLOCK, reach + rows + i * BLOCK, BLOCK, main + halo + i)
        for i in range(halo)
    ]
    for copy in copies:
        copy.start()
    arrange(gain, w_qkv, w_out, full_gain, wq, wkv, wo)
    for slot in range(SLOTS):
        spread[slot, :, :] = jnp.zeros(spread.shape[1:], spread.dtype)
        ones = lax.broadcasted_iota(jnp.int32, (16, spread.shape[2]), 0) == 0
        spread[slot, LANES + BIAS : LANES + BIAS + 16, :] = jnp.where(ones, 1.0, 0.0).astype(
            spread.dtype
        )

    def own_block(i, _):
        column = pl.multiple_of(reach + i * BLOCK, BLOCK)
        fetch(x, pl.multiple_of(i * BLOCK, BLOCK), column, BLOCK, i).wait()
        live = lambda n: live_ref[i * (BLOCK // WIN) + n]
        project(xq, column, full_gain, wq, wkv, store, live)
        return 0

    lax.fori_loop(0, main, own_block, 0)
    for i in range(2 * halo):
        copies[main + i].wait()
        column = i * BLOCK if i < halo else rows + i * BLOCK
        project(xq, column, full_gain, wq, wkv, store, queries=False)

    span = GROUP * WIN

    def send(i):
        at = i * span if isinstance(i, int) else pl.multiple_of(i * span, span)
        return pltpu.make_async_copy(
            xq.at[:, pl.ds(reach + at, span)], out.at[:, pl.ds(at, span)], sent.at[i]
        )

    def own_group(i, _):
        column = pl.multiple_of(reach + i * span, span)
        attend(column, i * GROUP, far_ref, xq, wo, store, far_rows, spread)
        send(i).start()
        return 0

    lax.fori_loop(0, rows // span, own_group, 0)
    for i in range(rows // span):
        send(i).wait()


def local(x, low, high, gain, w_qkv, w_out, counts, far):
    width, rows = x.shape
    reach = low.shape[1]
    total = rows + 2 * reach
    blocks = total // BLOCK
    bf16 = jnp.bfloat16
    any_space = pl.BlockSpec(memory_space=pl.ANY)
    smem, vmem = pl.BlockSpec(memory_space=pltpu.SMEM), pl.BlockSpec(memory_space=pltpu.VMEM)
    return pl.pallas_call(
        body,
        out_shape=jax.ShapeDtypeStruct((width, rows), bf16),
        in_specs=[smem, smem, any_space, any_space, any_space, vmem, vmem, vmem],
        out_specs=any_space,
        scratch_shapes=[
            pltpu.VMEM((total * PARTS + 2 * PAD, LANES), jnp.float32),
            pltpu.VMEM((width, total), bf16),
            pltpu.VMEM((SLOTS, WIN * PARTS, LANES), jnp.float32),
            pltpu.VMEM((SLOTS, 2 * LANES, HEADS * WIN), bf16),
            pltpu.VMEM((width, LANES), jnp.float32),
            pltpu.VMEM((width, width), bf16),
            pltpu.VMEM((width, PARTS * LANES), bf16),
            pltpu.VMEM((width, width), bf16),
            pltpu.SemaphoreType.DMA((blocks,)),
            pltpu.SemaphoreType.DMA((rows // (GROUP * WIN),)),
        ],
        compiler_params=pltpu.CompilerParams(vmem_limit_bytes=60 << 20),
    )(far, counts, x, low, high, gain, w_qkv, w_out)


def shards(points, gain, w_qkv, w_out, counts, far_index):
    rows, width = points.shape
    x = points.T
    count = lax.axis_size("gx")
    forward = [(i, i + 1) for i in range(count - 1)]
    backward = [(i + 1, i) for i in range(count - 1)]
    low = lax.ppermute(x[:, rows - REACH :], "gx", forward)
    high = lax.ppermute(x[:, :REACH], "gx", backward)
    return local(x, low, high, gain[None, :], w_qkv, w_out, counts, far_index).T


def solution(mesh):
    return jax.shard_map(
        shards,
        mesh=mesh,
        in_specs=(
            P(("tile", "gx"), None),
            P(),
            P(),
            P(),
            P(("tile", "gx")),
            P(("tile", "gx"), None),
        ),
        out_specs=P(("tile", "gx"), None),
        check_vma=False,
    )
```

```python
import functools
import math

import jax
import jax.numpy as jnp
from jax import lax
from jax.experimental import pallas as pl
from jax.experimental.pallas import tpu as pltpu
from jax.sharding import PartitionSpec as P

HEADS = 6
WIN = 128
REACH = 1024
LANES = 128
PARTS = 4
PAD = 2 * PARTS
BIAS = 64
DEAD = -1e30
BLOCK = 1024
SUB = 256
GROUP = 16
SLOTS = 4
PAIR = 2
EARLY, PREP, AHEAD, BEHIND, TAIL = 4, 3, 3, 3, 2


def pipelined(count, stages):
    for n in range(count + max(lag for _, lag in stages)):
        for run, lag in stages:
            if 0 <= n - lag < count:
                run(n - lag)


def project(xq, column, gain, wq, wkv, store, live=None, queries=True):
    width = xq.shape[0]
    norms, dots = {}, {}

    def norm(n):
        xf = xq[:, pl.ds(column + n * SUB, SUB)].astype(jnp.float32)
        mean = jnp.sum(xf, axis=0, keepdims=True) / width
        centred = xf - mean
        var = jnp.sum(centred * centred, axis=0, keepdims=True) / width
        scale = 1.0 / jnp.sqrt(var + 1e-05)
        full = jnp.concatenate([gain[...]] * (SUB // LANES), axis=1)
        norms[n] = (centred * scale * full).astype(jnp.bfloat16)

    def dot(n):
        normed = norms.pop(n)
        q = None
        if queries:
            q = jnp.dot(wq[...], normed, preferred_element_type=jnp.float32)
        kv = lax.dot_general(
            normed, wkv[...], (((0,), (0,)), ((), ())), preferred_element_type=jnp.float32
        )
        dots[n] = q, kv

    def keep(n):
        q, kv = dots.pop(n)
        if queries:
            xq[:, pl.ds(column + n * SUB, SUB)] = q.astype(jnp.bfloat16)
        kv = kv.astype(jnp.bfloat16).astype(jnp.float32)
        for part in range(PARTS):
            piece = kv[:, part * LANES : (part + 1) * LANES]
            if part == 1 and live is not None:
                lane = lax.broadcasted_iota(jnp.int32, (WIN, LANES), 1)
                slot = lax.broadcasted_iota(jnp.int32, (WIN, LANES), 0)
                bias = [
                    jnp.where((lane == BIAS) & (slot >= live(n * SUB // WIN + i)), DEAD, 0.0)
                    for i in range(SUB // WIN)
                ]
                piece = piece + jnp.concatenate(bias, axis=0)
            store[pl.ds(PAD + (column + n * SUB) * PARTS + part, SUB, stride=PARTS), :] = piece

    pipelined(BLOCK // SUB, ((norm, 0), (dot, 1), (keep, 2)))


def attend(count, column, window, far_ref, xq, w_out, store, far_rows, spread):
    width = xq.shape[0]
    head_dim = width // HEADS
    factor = math.log2(math.e) / math.sqrt(head_dim)
    per = HEADS // PAIR
    ready, pending, probs, mixed = {}, {}, {}, {}

    def gather(n):
        i, p = divmod(n, per)
        base = (pl.multiple_of(column + i * WIN, WIN) - REACH) * PARTS
        rows = far_rows.at[i % SLOTS]
        upper = lax.broadcasted_iota(jnp.int32, (2 * PARTS, LANES), 0) >= PARTS
        for j in range(p * WIN // per // 2 * 2, (p + 1) * WIN // per // 2 * 2, 2):
            one, two = [
                store[pl.ds(pl.multiple_of(at, PARTS), 2 * PARTS), :]
                for at in (
                    base + PAD + far_ref[window + i, j] * PARTS,
                    base + PAD - PARTS + far_ref[window + i, j + 1] * PARTS,
                )
            ]
            rows[pl.ds(j * PARTS, 2 * PARTS), :] = jnp.where(upper, two, one)

    def prepare(n):
        if n % per:
            return
        i = n // per
        own = pl.multiple_of(column + i * WIN, WIN)
        rows = far_rows.at[i % SLOTS]
        pieces = []
        for part in range(PARTS):
            dense = store[pl.ds(PAD + own * PARTS + part, WIN, stride=PARTS), :]
            far = rows[pl.ds(part, WIN, stride=PARTS), :]
            pieces.append(jnp.concatenate([dense, far], axis=0))
        keys = jnp.concatenate(pieces[:2], axis=1).astype(jnp.bfloat16)
        values = [pieces[2].T, pieces[3].T[: width - LANES]]
        values = jnp.concatenate(values, axis=0).astype(jnp.bfloat16)
        q = xq[:, pl.ds(own, WIN)]
        for h in range(HEADS):
            head = slice(h * head_dim, (h + 1) * head_dim)
            spread[i % SLOTS, head, h * WIN : (h + 1) * WIN] = q[head]
        ready[i] = keys, values

    def score(n):
        i, p = divmod(n, per)
        pending[n] = jnp.dot(
            ready[i][0],
            spread[i % SLOTS, :, p * PAIR * WIN : (p + 1) * PAIR * WIN],
            preferred_element_type=jnp.float32,
        )

    def softmax(n):
        s2 = pending.pop(n)
        halves = []
        for h in range(PAIR):
            s = s2[:, h * WIN : (h + 1) * WIN]
            top = jnp.max(s, axis=0, keepdims=True)
            expo = jnp.exp2((s - top) * factor)
            inverse = 1.0 / jnp.sum(expo, axis=0, keepdims=True)
            halves.append((expo * inverse).astype(jnp.bfloat16))
        probs[n] = jnp.concatenate(halves, axis=1)

    def blend(n):
        i, p = divmod(n, per)
        out = jnp.dot(
            ready[i][1][p * PAIR * head_dim : (p + 1) * PAIR * head_dim],
            probs.pop(n),
            preferred_element_type=jnp.float32,
        )
        for h in range(PAIR):
            piece = out[h * head_dim : (h + 1) * head_dim, h * WIN : (h + 1) * WIN]
            mixed.setdefault(i, []).append(piece)

    def finish(n):
        i, p = divmod(n, per)
        if p < per - 1:
            return
        m = jnp.concatenate(mixed.pop(i), axis=0).astype(jnp.bfloat16)
        out = jnp.dot(w_out[...], m, preferred_element_type=jnp.float32)
        xq[:, pl.ds(column + i * WIN, WIN)] = out.astype(jnp.bfloat16)

    lags = [EARLY, PREP, AHEAD, BEHIND, TAIL]
    lags = [sum(lags[:i]) for i in range(6)]
    pipelined(count * per, tuple(zip((gather, prepare, score, softmax, blend, finish), lags)))


def arrange(gain, w_qkv, w_out, full_gain, wq, wkv, wo):
    width = w_qkv.shape[0]
    f32 = jnp.float32
    full_gain[...] = jnp.broadcast_to(gain[...], (LANES, width)).T
    w = w_qkv[...].astype(f32)
    wq[...] = w[:, :width].T.astype(wq.dtype)
    wo[...] = w_out[...].astype(f32).T.astype(wo.dtype)
    pad = jnp.zeros((width, 2 * LANES - width), f32)
    parts = []
    for first in (width, 2 * width):
        parts += [w[:, first : first + width], pad]
    wkv[...] = jnp.concatenate(parts, axis=1).astype(wkv.dtype)


def clear(spread):
    for slot in range(SLOTS):
        spread[slot, :, :] = jnp.zeros(spread.shape[1:], spread.dtype)
        ones = lax.broadcasted_iota(jnp.int32, (16, spread.shape[2]), 0) == 0
        spread[slot, LANES + BIAS : LANES + BIAS + 16, :] = jnp.where(ones, 1.0, 0.0).astype(
            spread.dtype
        )


def inner_body(
    group, far_ref, live_ref, x, gain, w_qkv, w_out, out, edge_rows, edge_q,
    store, xq, far_rows, spread, full_gain, wq, wkv, wo, got, sent, kept,
):
    rows = x.shape[1]
    blocks, span = rows // BLOCK, group * WIN
    groups = (rows - 2 * REACH) // span

    def fetch(i):
        cut = pl.ds(i * BLOCK if isinstance(i, int) else pl.multiple_of(i * BLOCK, BLOCK), BLOCK)
        return pltpu.make_async_copy(x.at[:, cut], xq.at[:, cut], got.at[i])

    for i in range(blocks):
        fetch(i).start()
    arrange(gain, w_qkv, w_out, full_gain, wq, wkv, wo)
    clear(spread)

    def block(i, _):
        fetch(i).wait()
        live = lambda n: live_ref[i * (BLOCK // WIN) + n]
        project(xq, pl.multiple_of(i * BLOCK, BLOCK), full_gain, wq, wkv, store, live)
        return 0

    lax.fori_loop(0, blocks, block, 0)
    size = 2 * REACH * PARTS
    copies = []
    for side in range(2):
        copies.append(
            pltpu.make_async_copy(
                store.at[pl.ds(PAD + side * (rows * PARTS - size), size)],
                edge_rows.at[pl.ds(side * size, size)],
                kept.at[side],
            )
        )
        copies.append(
            pltpu.make_async_copy(
                xq.at[:, pl.ds(side * (rows - REACH), REACH)],
                edge_q.at[:, pl.ds(side * REACH, REACH)],
                kept.at[2 + side],
            )
        )
    for copy in copies:
        copy.start()

    def send(i):
        at = REACH + (i * span if isinstance(i, int) else pl.multiple_of(i * span, span))
        cut = pl.ds(at, span)
        return pltpu.make_async_copy(xq.at[:, cut], out.at[:, cut], sent.at[i])

    def some(i, _):
        column = pl.multiple_of(REACH + i * span, WIN)
        attend(
            group, column, REACH // WIN + i * group, far_ref, xq, wo, store, far_rows, spread
        )
        send(i).start()
        return 0

    lax.fori_loop(0, groups, some, 0)
    for i in range(groups):
        send(i).wait()
    for copy in copies:
        copy.wait()


def edge_body(
    far_ref, inner, low, high, edge_rows, edge_q, gain, w_qkv, w_out, out,
    store, xq, far_rows, spread, full_gain, wq, wkv, wo, got, sent,
):
    rows = out.shape[1]
    count, segment = REACH // WIN, 3 * REACH
    size = 2 * REACH * PARTS
    halos, copies = (0, 2 * segment - REACH), []
    for side, halo in enumerate((low, high)):
        copies.append(
            pltpu.make_async_copy(halo, xq.at[:, pl.ds(halos[side], REACH)], got.at[side])
        )
        copies.append(
            pltpu.make_async_copy(
                edge_q.at[:, pl.ds(side * REACH, REACH)],
                xq.at[:, pl.ds(side * segment + REACH, REACH)],
                got.at[2 + side],
            )
        )
        copies.append(
            pltpu.make_async_copy(
                edge_rows.at[pl.ds(side * size, size)],
                store.at[pl.ds(PAD + (REACH + side * 2 * REACH) * PARTS, size)],
                got.at[4 + side],
            )
        )
    for copy in copies:
        copy.start()
    arrange(gain, w_qkv, w_out, full_gain, wq, wkv, wo)
    clear(spread)
    for copy in copies[0::3]:
        copy.wait()

    def halo_block(i, _):
        column = pl.multiple_of(i * (2 * segment - REACH), BLOCK)
        project(xq, column, full_gain, wq, wkv, store, queries=False)
        return 0

    lax.fori_loop(0, 2, halo_block, 0)
    for copy in copies[1::3] + copies[2::3]:
        copy.wait()

    def send(side):
        return pltpu.make_async_copy(
            xq.at[:, pl.ds(side * segment + REACH, REACH)],
            out.at[:, pl.ds(side * (rows - REACH), REACH)],
            sent.at[side],
        )

    def end(side, _):
        column = pl.multiple_of(side * segment + REACH, WIN)
        window = side * (rows // WIN - count)
        attend(count, column, window, far_ref, xq, wo, store, far_rows, spread)
        return 0

    lax.fori_loop(0, 2, end, 0)
    for side in range(2):
        send(side).start()
    for side in range(2):
        send(side).wait()


def scratch(width, total):
    bf16 = jnp.bfloat16
    return [
        pltpu.VMEM((total * PARTS + 2 * PAD, LANES), jnp.float32),
        pltpu.VMEM((width, total), bf16),
        pltpu.VMEM((SLOTS, WIN * PARTS, LANES), jnp.float32),
        pltpu.VMEM((SLOTS, 2 * LANES, HEADS * WIN), bf16),
        pltpu.VMEM((width, LANES), jnp.float32),
        pltpu.VMEM((width, width), bf16),
        pltpu.VMEM((width, PARTS * LANES), bf16),
        pltpu.VMEM((width, width), bf16),
    ]


def strip(x, halo, gain, w_qkv, w_out, counts, far):
    width, rows = x.shape
    bf16 = jnp.bfloat16
    hbm = pl.BlockSpec(memory_space=pl.ANY)
    smem, vmem = pl.BlockSpec(memory_space=pltpu.SMEM), pl.BlockSpec(memory_space=pltpu.VMEM)
    group = math.gcd((rows - 2 * REACH) // WIN, GROUP)
    flops = 2 * rows * width * (4 * width + 4 * WIN)
    whole = jax.ShapeDtypeStruct((width, rows), bf16)
    inner, edge_rows, edge_q = pl.pallas_call(
        functools.partial(inner_body, group),
        out_shape=(
            whole,
            jax.ShapeDtypeStruct((4 * REACH * PARTS, LANES), jnp.float32),
            jax.ShapeDtypeStruct((width, 2 * REACH), bf16),
        ),
        in_specs=[smem, smem, hbm, vmem, vmem, vmem],
        out_specs=(hbm, hbm, hbm),
        scratch_shapes=scratch(width, rows)
        + [
            pltpu.SemaphoreType.DMA((rows // BLOCK,)),
            pltpu.SemaphoreType.DMA(((rows - 2 * REACH) // (group * WIN),)),
            pltpu.SemaphoreType.DMA((4,)),
        ],
        compiler_params=pltpu.CompilerParams(vmem_limit_bytes=60 << 20),
        cost_estimate=pl.CostEstimate(
            flops=flops, bytes_accessed=6 * rows * width, transcendentals=2 * rows * WIN * HEADS
        ),
        name="inner",
    )(far, counts, x, gain, w_qkv, w_out)
    low, high = halo
    return pl.pallas_call(
        edge_body,
        out_shape=whole,
        in_specs=[smem, hbm, hbm, hbm, hbm, hbm, vmem, vmem, vmem],
        out_specs=hbm,
        input_output_aliases={1: 0},
        scratch_shapes=scratch(width, 6 * REACH)
        + [pltpu.SemaphoreType.DMA((6,)), pltpu.SemaphoreType.DMA((2,))],
        compiler_params=pltpu.CompilerParams(vmem_limit_bytes=60 << 20),
        name="edge",
    )(far, inner, low, high, edge_rows, edge_q, gain, w_qkv, w_out)


def shards(points, gain, w_qkv, w_out, counts, far_index):
    rows, width = points.shape
    x = points.T
    count = lax.axis_size("gx")
    forward = [(i, i + 1) for i in range(count - 1)]
    backward = [(i + 1, i) for i in range(count - 1)]
    low = lax.ppermute(x[:, rows - REACH :], "gx", forward)
    high = lax.ppermute(x[:, :REACH], "gx", backward)
    return strip(x, (low, high), gain[None, :], w_qkv, w_out, counts, far_index).T


def solution(mesh):
    return jax.shard_map(
        shards,
        mesh=mesh,
        in_specs=(
            P(("tile", "gx"), None),
            P(),
            P(),
            P(),
            P(("tile", "gx")),
            P(("tile", "gx"), None),
        ),
        out_specs=P(("tile", "gx"), None),
        check_vma=False,
    )
```

```python
import functools
import math

import jax
import jax.numpy as jnp
from jax import lax
from jax.experimental import pallas as pl
from jax.experimental.pallas import tpu as pltpu
from jax.sharding import PartitionSpec as P

HEADS = 6
WIN = 128
REACH = 1024
LANES = 128
PARTS = 4
PAD = 2 * PARTS
BIAS = 64
DEAD = -1e30
BLOCK = 1024
SUB = 256
GROUP = 16
CHUNK = 16
SLOTS = 4
PAIR = 2
EARLY, PREP, AHEAD, BEHIND, TAIL = 4, 3, 3, 3, 2


def pipelined(count, stages):
    for n in range(count + max(lag for _, lag in stages)):
        for run, lag in stages:
            if 0 <= n - lag < count:
                run(n - lag)


def project(xq, column, gain, wq, wkv, store, live=None, queries=True):
    width = xq.shape[0]
    norms, dots = {}, {}

    def norm(n):
        xf = xq[:, pl.ds(column + n * SUB, SUB)].astype(jnp.float32)
        mean = jnp.sum(xf, axis=0, keepdims=True) / width
        centred = xf - mean
        var = jnp.sum(centred * centred, axis=0, keepdims=True) / width
        scale = 1.0 / jnp.sqrt(var + 1e-05)
        full = jnp.concatenate([gain[...]] * (SUB // LANES), axis=1)
        norms[n] = (centred * scale * full).astype(jnp.bfloat16)

    def dot(n):
        normed = norms.pop(n)
        q = None
        if queries:
            q = jnp.dot(wq[...], normed, preferred_element_type=jnp.float32)
        kv = lax.dot_general(
            normed, wkv[...], (((0,), (0,)), ((), ())), preferred_element_type=jnp.float32
        )
        dots[n] = q, kv

    def keep(n):
        q, kv = dots.pop(n)
        if queries:
            xq[:, pl.ds(column + n * SUB, SUB)] = q.astype(jnp.bfloat16)
        kv = kv.astype(jnp.bfloat16).astype(jnp.float32)
        for part in range(PARTS):
            piece = kv[:, part * LANES : (part + 1) * LANES]
            if part == 1 and live is not None:
                lane = lax.broadcasted_iota(jnp.int32, (WIN, LANES), 1)
                slot = lax.broadcasted_iota(jnp.int32, (WIN, LANES), 0)
                bias = [
                    jnp.where((lane == BIAS) & (slot >= live(n * SUB // WIN + i)), DEAD, 0.0)
                    for i in range(SUB // WIN)
                ]
                piece = piece + jnp.concatenate(bias, axis=0)
            store[pl.ds(PAD + (column + n * SUB) * PARTS + part, SUB, stride=PARTS), :] = piece

    pipelined(BLOCK // SUB, ((norm, 0), (dot, 1), (keep, 2)))


def attend(count, column, window, far_ref, xq, w_out, store, far_rows, spread):
    width = xq.shape[0]
    head_dim = width // HEADS
    factor = math.log2(math.e) / math.sqrt(head_dim)
    per = HEADS // PAIR
    ready, pending, probs, mixed = {}, {}, {}, {}

    def gather(n):
        i, p = divmod(n, per)
        base = (pl.multiple_of(column + i * WIN, WIN) - REACH) * PARTS
        rows = far_rows.at[i % SLOTS]
        upper = lax.broadcasted_iota(jnp.int32, (2 * PARTS, LANES), 0) >= PARTS
        for j in range(p * WIN // per // 2 * 2, (p + 1) * WIN // per // 2 * 2, 2):
            one, two = [
                store[pl.ds(pl.multiple_of(at, PARTS), 2 * PARTS), :]
                for at in (
                    base + PAD + far_ref[window + i, j] * PARTS,
                    base + PAD - PARTS + far_ref[window + i, j + 1] * PARTS,
                )
            ]
            rows[pl.ds(j * PARTS, 2 * PARTS), :] = jnp.where(upper, two, one)

    def prepare(n):
        if n % per:
            return
        i = n // per
        own = pl.multiple_of(column + i * WIN, WIN)
        rows = far_rows.at[i % SLOTS]
        pieces = []
        for part in range(PARTS):
            dense = store[pl.ds(PAD + own * PARTS + part, WIN, stride=PARTS), :]
            far = rows[pl.ds(part, WIN, stride=PARTS), :]
            pieces.append(jnp.concatenate([dense, far], axis=0))
        keys = jnp.concatenate(pieces[:2], axis=1).astype(jnp.bfloat16)
        values = [pieces[2].T, pieces[3].T[: width - LANES]]
        values = jnp.concatenate(values, axis=0).astype(jnp.bfloat16)
        q = xq[:, pl.ds(own, WIN)]
        for h in range(HEADS):
            head = slice(h * head_dim, (h + 1) * head_dim)
            spread[i % SLOTS, head, h * WIN : (h + 1) * WIN] = q[head]
        ready[i] = keys, values

    def score(n):
        i, p = divmod(n, per)
        pending[n] = jnp.dot(
            ready[i][0],
            spread[i % SLOTS, :, p * PAIR * WIN : (p + 1) * PAIR * WIN],
            preferred_element_type=jnp.float32,
        )

    def softmax(n):
        s2 = pending.pop(n)
        halves = []
        for h in range(PAIR):
            head = s2[:, h * WIN : (h + 1) * WIN]
            cut = [head[c : c + CHUNK] for c in range(0, 2 * WIN, CHUNK)]
            top = cut[0]
            for c in cut[1:]:
                top = jnp.maximum(top, c)
            top = jnp.max(top, axis=0, keepdims=True)
            expo, total = [], 0.0
            for c in cut:
                e = jnp.exp2((c - top) * factor)
                expo.append(e)
                total = total + e
            inverse = 1.0 / jnp.sum(total, axis=0, keepdims=True)
            prob = [(e * inverse).astype(jnp.bfloat16) for e in expo]
            halves.append(jnp.concatenate(prob, axis=0))
        probs[n] = jnp.concatenate(halves, axis=1)

    def blend(n):
        i, p = divmod(n, per)
        out = jnp.dot(
            ready[i][1][p * PAIR * head_dim : (p + 1) * PAIR * head_dim],
            probs.pop(n),
            preferred_element_type=jnp.float32,
        )
        for h in range(PAIR):
            piece = out[h * head_dim : (h + 1) * head_dim, h * WIN : (h + 1) * WIN]
            mixed.setdefault(i, []).append(piece)

    def finish(n):
        i, p = divmod(n, per)
        if p < per - 1:
            return
        m = jnp.concatenate(mixed.pop(i), axis=0).astype(jnp.bfloat16)
        out = jnp.dot(w_out[...], m, preferred_element_type=jnp.float32)
        xq[:, pl.ds(column + i * WIN, WIN)] = out.astype(jnp.bfloat16)

    lags = [EARLY, PREP, AHEAD, BEHIND, TAIL]
    lags = [sum(lags[:i]) for i in range(6)]
    pipelined(count * per, tuple(zip((gather, prepare, score, softmax, blend, finish), lags)))


def arrange(gain, w_qkv, w_out, full_gain, wq, wkv, wo):
    width = w_qkv.shape[0]
    f32 = jnp.float32
    full_gain[...] = jnp.broadcast_to(gain[...], (LANES, width)).T
    w = w_qkv[...].astype(f32)
    wq[...] = w[:, :width].T.astype(wq.dtype)
    wo[...] = w_out[...].astype(f32).T.astype(wo.dtype)
    pad = jnp.zeros((width, 2 * LANES - width), f32)
    parts = []
    for first in (width, 2 * width):
        parts += [w[:, first : first + width], pad]
    wkv[...] = jnp.concatenate(parts, axis=1).astype(wkv.dtype)


def clear(spread):
    for slot in range(SLOTS):
        spread[slot, :, :] = jnp.zeros(spread.shape[1:], spread.dtype)
        ones = lax.broadcasted_iota(jnp.int32, (16, spread.shape[2]), 0) == 0
        spread[slot, LANES + BIAS : LANES + BIAS + 16, :] = jnp.where(ones, 1.0, 0.0).astype(
            spread.dtype
        )


def load(sems, *pairs):
    copies = [
        pltpu.make_async_copy(src, dst, sems.at[i]) for i, (src, dst) in enumerate(pairs)
    ]
    for copy in copies:
        copy.start()
    return copies


def inner_body(
    group, far, counts, x, gain_in, w_qkv_in, w_out_in, out, edge_rows, edge_q,
    store, xq, far_rows, spread, full_gain, wq, wkv, wo, gain, w_qkv, w_out, far_ref,
    loaded, live_ref, got, sent, kept,
):
    rows = x.shape[1]
    blocks, span = rows // BLOCK, group * WIN
    groups = (rows - 2 * REACH) // span

    def fetch(i):
        cut = pl.ds(i * BLOCK if isinstance(i, int) else pl.multiple_of(i * BLOCK, BLOCK), BLOCK)
        return pltpu.make_async_copy(x.at[:, cut], xq.at[:, cut], got.at[i])

    loads = load(
        loaded, (gain_in, gain), (w_qkv_in, w_qkv), (w_out_in, w_out), (far, far_ref),
        (counts, live_ref),
    )
    for i in range(blocks):
        fetch(i).start()
    clear(spread)
    for copy in loads[:3]:
        copy.wait()
    arrange(gain, w_qkv, w_out, full_gain, wq, wkv, wo)
    for copy in loads[3:]:
        copy.wait()

    def block(i, _):
        fetch(i).wait()
        live = lambda n: live_ref[i * (BLOCK // WIN) + n]
        project(xq, pl.multiple_of(i * BLOCK, BLOCK), full_gain, wq, wkv, store, live)
        return 0

    lax.fori_loop(0, blocks, block, 0)
    size = 2 * REACH * PARTS
    copies = []
    for side in range(2):
        copies.append(
            pltpu.make_async_copy(
                store.at[pl.ds(PAD + side * (rows * PARTS - size), size)],
                edge_rows.at[pl.ds(side * size, size)],
                kept.at[side],
            )
        )
        copies.append(
            pltpu.make_async_copy(
                xq.at[:, pl.ds(side * (rows - REACH), REACH)],
                edge_q.at[:, pl.ds(side * REACH, REACH)],
                kept.at[2 + side],
            )
        )
    for copy in copies:
        copy.start()

    def send(i):
        at = REACH + (i * span if isinstance(i, int) else pl.multiple_of(i * span, span))
        cut = pl.ds(at, span)
        return pltpu.make_async_copy(xq.at[:, cut], out.at[:, cut], sent.at[i])

    def some(i, _):
        column = pl.multiple_of(REACH + i * span, WIN)
        attend(
            group, column, REACH // WIN + i * group, far_ref, xq, wo, store, far_rows, spread
        )
        send(i).start()
        return 0

    lax.fori_loop(0, groups, some, 0)
    for i in range(groups):
        send(i).wait()
    for copy in copies:
        copy.wait()


def edge_body(
    far, inner, low, high, edge_rows, edge_q, gain_in, w_qkv_in, w_out_in, out,
    store, xq, far_rows, spread, full_gain, wq, wkv, wo, gain, w_qkv, w_out, far_ref,
    loaded, got, sent,
):
    rows = out.shape[1]
    count, segment = REACH // WIN, 3 * REACH
    size = 2 * REACH * PARTS
    windows = rows // WIN
    halos, rest, parts = [], [], []
    for side, halo in enumerate((low, high)):
        column = side * (2 * segment - REACH)
        halos.append((halo, xq.at[:, pl.ds(column, REACH)]))
        cut = pl.ds(side * (windows - count), count)
        parts.append((far.at[cut], far_ref.at[pl.ds(side * count, count)]))
        cut = pl.ds(side * REACH, REACH)
        rest.append((edge_q.at[:, cut], xq.at[:, pl.ds(side * segment + REACH, REACH)]))
        rows_at = PAD + (REACH + side * 2 * REACH) * PARTS
        rest.append((edge_rows.at[pl.ds(side * size, size)], store.at[pl.ds(rows_at, size)]))
    loads = load(
        loaded, (gain_in, gain), (w_qkv_in, w_qkv), (w_out_in, w_out), *halos, *parts
    )
    copies = load(got, *rest)
    clear(spread)
    for copy in loads[:3]:
        copy.wait()
    arrange(gain, w_qkv, w_out, full_gain, wq, wkv, wo)
    for copy in loads[3:]:
        copy.wait()

    def halo_block(i, _):
        column = pl.multiple_of(i * (2 * segment - REACH), BLOCK)
        project(xq, column, full_gain, wq, wkv, store, queries=False)
        return 0

    lax.fori_loop(0, 2, halo_block, 0)
    for copy in copies:
        copy.wait()

    def send(side):
        source = pl.multiple_of(side * segment + REACH, WIN)
        target = pl.multiple_of(side * (rows - REACH), WIN)
        return pltpu.make_async_copy(
            xq.at[:, pl.ds(source, REACH)], out.at[:, pl.ds(target, REACH)], sent.at[side]
        )

    def end(side, _):
        column = pl.multiple_of(side * segment + REACH, WIN)
        attend(count, column, side * count, far_ref, xq, wo, store, far_rows, spread)
        send(side).start()
        return 0

    lax.fori_loop(0, 2, end, 0)
    for side in range(2):
        send(side).wait()


def scratch(width, total, far_rows, loads):
    bf16 = jnp.bfloat16
    return [
        pltpu.VMEM((total * PARTS + 2 * PAD, LANES), jnp.float32),
        pltpu.VMEM((width, total), bf16),
        pltpu.VMEM((SLOTS, WIN * PARTS, LANES), jnp.float32),
        pltpu.VMEM((SLOTS, 2 * LANES, HEADS * WIN), bf16),
        pltpu.VMEM((width, LANES), jnp.float32),
        pltpu.VMEM((width, width), bf16),
        pltpu.VMEM((width, PARTS * LANES), bf16),
        pltpu.VMEM((width, width), bf16),
        pltpu.VMEM((1, width), jnp.float32),
        pltpu.VMEM((width, 3 * width), bf16),
        pltpu.VMEM((width, width), bf16),
        pltpu.SMEM((far_rows, WIN), jnp.int32),
        pltpu.SemaphoreType.DMA((loads,)),
    ]


def strip(x, halo, gain, w_qkv, w_out, counts, far):
    width, rows = x.shape
    bf16 = jnp.bfloat16
    hbm = pl.BlockSpec(memory_space=pl.ANY)
    group = math.gcd((rows - 2 * REACH) // WIN, GROUP)
    flops = 2 * rows * width * (4 * width + 4 * WIN)
    whole = jax.ShapeDtypeStruct((width, rows), bf16)
    inner, edge_rows, edge_q = pl.pallas_call(
        functools.partial(inner_body, group),
        out_shape=(
            whole,
            jax.ShapeDtypeStruct((4 * REACH * PARTS, LANES), jnp.float32),
            jax.ShapeDtypeStruct((width, 2 * REACH), bf16),
        ),
        in_specs=[hbm] * 6,
        out_specs=(hbm, hbm, hbm),
        scratch_shapes=scratch(width, rows, rows // WIN, 5)
        + [
            pltpu.SMEM((rows // WIN,), jnp.int32),
            pltpu.SemaphoreType.DMA((rows // BLOCK,)),
            pltpu.SemaphoreType.DMA(((rows - 2 * REACH) // (group * WIN),)),
            pltpu.SemaphoreType.DMA((4,)),
        ],
        compiler_params=pltpu.CompilerParams(vmem_limit_bytes=60 << 20),
        cost_estimate=pl.CostEstimate(
            flops=flops, bytes_accessed=6 * rows * width, transcendentals=2 * rows * WIN * HEADS
        ),
        name="inner",
    )(far, counts, x, gain, w_qkv, w_out)
    low, high = halo
    return pl.pallas_call(
        edge_body,
        out_shape=whole,
        in_specs=[hbm] * 9,
        out_specs=hbm,
        input_output_aliases={1: 0},
        scratch_shapes=scratch(width, 6 * REACH, 2 * REACH // WIN, 7)
        + [pltpu.SemaphoreType.DMA((4,)), pltpu.SemaphoreType.DMA((2,))],
        compiler_params=pltpu.CompilerParams(vmem_limit_bytes=60 << 20),
        name="edge",
    )(far, inner, low, high, edge_rows, edge_q, gain, w_qkv, w_out)


def shards(points, gain, w_qkv, w_out, counts, far_index):
    rows, width = points.shape
    x = points.T
    count = lax.axis_size("gx")
    forward = [(i, i + 1) for i in range(count - 1)]
    backward = [(i + 1, i) for i in range(count - 1)]
    low = lax.ppermute(x[:, rows - REACH :], "gx", forward)
    high = lax.ppermute(x[:, :REACH], "gx", backward)
    return strip(x, (low, high), gain[None, :], w_qkv, w_out, counts, far_index).T


def solution(mesh):
    return jax.shard_map(
        shards,
        mesh=mesh,
        in_specs=(
            P(("tile", "gx"), None),
            P(),
            P(),
            P(),
            P(("tile", "gx")),
            P(("tile", "gx"), None),
        ),
        out_specs=P(("tile", "gx"), None),
        check_vma=False,
    )
```
